256 devices in a mesh: pair: 64 (over y, z, x_lo), sec: 4 (over x_hi, core).
Axes of the slice: x: 4 (x_hi: 2, x_lo: 2; x = x_hi * 2 + x_lo), y: 4, z: 8, core: 2. Of those that a mesh axis runs over, the one named last changes fastest.
Arguments:
- psi: bfloat16 [32, 768, 384], P('sec'), may hold values from -6 to 6
- sec_rows: int32 [32], replicated, may hold values from 128 to 768, as said below
- match: int32 [32], replicated, may hold values from 0 to 31, each once
- normal_ops: bfloat16 [64, 32, 768, 768], P('pair', 'sec'), may hold values from -0.02734375 to 0.02734375
- comp_ops: bfloat16 [64, 32, 384, 384], P('pair', 'sec'), may hold values from -0.3125 to 0.3125
Outputs:
- sigma: bfloat16 [32, 768, 384], P('sec', 'pair')
The draws below stay inside these ranges and needn't reach their ends.
Inputs may be any that keep to these rules, and one draw needn't show every extreme that they name: `sec_rows`: every entry is a multiple of 128; some entry equals 768 in every draw.
All inputs are finite; a program needn't handle non-finite values.
Results may differ from the reference program's by a relative error of at most 0.0049.
Values may be sent and summed in bfloat16 or wider, within the bound.
No kernel may reach another device: no remote copies, remote signals or barrier semaphores. Data moves between devices by JAX's collectives and lax.ppermute only.
A program may use at most 128 MiB of HBM per device.

```python
import jax
import jax.numpy as jnp
from jax import lax

MB = 768
NB = 384
ROW_UNIT = 128
SECTORS = 32
PAIRS = 64


def draw_sec_rows(key, part):
    units = MB // ROW_UNIT
    first_key, second_key = jax.random.split(key)
    counts = jax.random.randint(first_key, (SECTORS,), 1, units + 1) * ROW_UNIT
    where_full = jax.random.randint(second_key, (), 0, SECTORS)
    return jnp.where(jnp.arange(SECTORS) == where_full, MB, counts).astype(jnp.int32)


def steps_of(rng, shape, cuts, smallest, top_value):
    def one(position, blocks):
        draws = jax.random.uniform(jax.random.fold_in(jax.random.fold_in(rng, 6), position), (blocks,), jnp.float32, smallest / len(cuts), top_value / len(cuts))
        return jnp.repeat(jnp.exp(draws), shape[position] // blocks).reshape((-1,) + (1,) * (len(shape) - position - 1))

    gain = one(*cuts[0])
    for cut in cuts[1:]:
        gain = gain * one(*cut)
    return gain


def normal_values(rng, extent, scale, reach, cuts=(), kind=jnp.bfloat16):
    level = steps_of(rng, extent, cuts, -0.22, 0.18) if cuts else 1.0
    entries = jax.random.normal(rng, extent, jnp.float32) * scale * level
    return jnp.minimum(jnp.maximum(entries, -reach), reach).astype(kind)


def setup_inputs(seed: int = 0) -> dict:
    keys = jax.random.split(jax.random.key(seed), 6)
    return {
        "psi": normal_values(keys[0], (SECTORS, MB, NB), 1.0, 6.0, ((0, 4),)),
        "sec_rows": draw_sec_rows(jax.random.fold_in(keys[5], 71), 0),
        "match": jax.random.permutation(keys[2], SECTORS).astype(jnp.int32),
        "normal_ops": normal_values(keys[3], (PAIRS, SECTORS, MB, MB), (MB * PAIRS) ** -0.5, 0.02734375, ((0, 64), (1, 4))),
        "comp_ops": normal_values(keys[4], (PAIRS, SECTORS, NB, NB), NB ** -0.5, 0.3125, ((0, 64), (1, 4))),
    }


def reference(psi, sec_rows, match, normal_ops, comp_ops):
    line = jnp.arange(MB, dtype=jnp.int32)
    keep = line[None, :] < sec_rows[:, None]
    kept = jnp.where(keep[:, :, None], psi, jnp.zeros_like(psi))
    kept_wide = kept.astype(jnp.float32)

    def one_pair(total, index):
        left_op = normal_ops[index].astype(jnp.float32)
        right_op = comp_ops[PAIRS - 1 - index].astype(jnp.float32)
        half = jnp.einsum('sab,sbc->sac', left_op, kept_wide).astype(jnp.bfloat16)
        term = jnp.einsum('sac,sdc->sad', half.astype(jnp.float32), right_op)
        return total + term, None

    start = jnp.zeros((SECTORS, MB, NB), jnp.float32)
    images, _ = lax.scan(one_pair, start, jnp.arange(PAIRS, dtype=jnp.int32))
    placed = jnp.zeros((SECTORS, MB, NB), jnp.float32).at[match].set(images)
    out_keep = line[None, :] < sec_rows[:, None]
    placed = jnp.where(out_keep[:, :, None], placed, jnp.zeros_like(placed))
    return placed.astype(jnp.bfloat16)
```

```python
import jax
import jax.numpy as jnp
from jax import lax
from jax.experimental import pallas as pl
from jax.experimental.pallas import tpu as pltpu
from jax.sharding import PartitionSpec as P


INTERPRET = False
YS, ZS, XS = 4, 8, 2
CHUNK = 2


def plane_perm(dy, dx):
    out = []
    for p in range(YS * ZS * XS):
        y, z, x = p // (ZS * XS), (p // XS) % ZS, p % XS
        out.append((p, ((y + dy) % YS) * ZS * XS + z * XS + (x ^ dx)))
    return out


def line_perm(dz):
    out = []
    for p in range(YS * ZS * XS):
        y, z, x = p // (ZS * XS), (p // XS) % ZS, p % XS
        out.append((p, y * ZS * XS + ((z + dz) % ZS) * XS + x))
    return out


def pick_sources(gathered, match, targets):
    total = match.shape[0]
    hits = match[None, :] == targets[:, None]
    source = jnp.sum(jnp.where(hits, jnp.arange(total, dtype=jnp.int32)[None, :], 0), axis=1)
    return gathered[source]


def terms_kernel(half_ref, comp_ref, own_ref, *send_refs):
    total = lax.dot_general(
        half_ref[0], comp_ref[0], (((1,), (1,)), ((), ())), preferred_element_type=jnp.float32
    )
    rows = own_ref.shape[1]
    own_ref[0] = total[:rows]
    for index, ref in enumerate(send_refs):
        ref[0] = total[(index + 1) * rows : (index + 2) * rows].astype(ref.dtype)


def terms_of(half, comp):
    sectors, rows, cols = half.shape
    part = rows // (YS * XS)
    spec = pl.BlockSpec((1, part, cols), lambda s: (s, 0, 0))
    others = YS * XS - 1
    return pl.pallas_call(
        terms_kernel,
        grid=(sectors,),
        in_specs=[
            pl.BlockSpec((1, rows, cols), lambda s: (s, 0, 0)),
            pl.BlockSpec((1, cols, cols), lambda s: (s, 0, 0)),
        ],
        out_specs=[spec] * (others + 1),
        out_shape=[jax.ShapeDtypeStruct((sectors, part, cols), jnp.float32)]
        + [jax.ShapeDtypeStruct((sectors, part, cols), jnp.bfloat16)] * others,
        interpret=INTERPRET,
        name="terms",
    )(half, comp)


def shards(psi, sec_rows, match, normal_ops, comp_ops):
    sec_dev, block_rows, cols = psi.shape
    pairs = lax.axis_size("pair")
    share = block_rows // pairs
    first = lax.axis_index("sec") * sec_dev
    pair = lax.axis_index("pair")
    targets = first + jnp.arange(sec_dev, dtype=jnp.int32)
    rows_here = lax.dynamic_slice_in_dim(sec_rows, first, sec_dev)

    mirror = [(p, pairs - 1 - p) for p in range(pairs)]
    starts = list(range(0, sec_dev, CHUNK))
    mirrored = [lax.ppermute(comp_ops[0, s : s + CHUNK], "pair", mirror) for s in starts]

    line = jnp.arange(block_rows, dtype=jnp.int32)
    kept = jnp.where((line[None, :] < rows_here[:, None])[:, :, None], psi, jnp.zeros_like(psi))
    half = jnp.einsum(
        "sab,sbc->sac", normal_ops[0], kept, preferred_element_type=jnp.float32
    ).astype(jnp.bfloat16)
    y, z, x = pair // (ZS * XS), (pair // XS) % ZS, pair % XS
    part = block_rows // (YS * XS)
    block, inner = line // part, line % part
    row = share * (
        ((y + block // XS) % YS) * (ZS * XS)
        + ((z + inner // share) % ZS) * XS
        + (x ^ (block % XS))
    ) + inner % share
    order = (row[:, None] == line[None, :]).astype(jnp.bfloat16)
    half = jnp.einsum("ia,sac->sic", order, half, preferred_element_type=jnp.float32).astype(
        jnp.bfloat16
    )

    pieces = []
    for s, comp in zip(starts, mirrored):
        own, *sends = terms_of(half[s : s + CHUNK], comp)
        total = own
        for index, value in enumerate(sends):
            block_id = index + 1
            got = lax.ppermute(value, "pair", plane_perm(block_id // XS, block_id % XS))
            total = total + got.astype(jnp.float32)
        pieces.append(total)
    mine = jnp.concatenate(pieces, axis=0)
    mine = mine.reshape(sec_dev, ZS, share, cols).transpose(1, 0, 2, 3)
    mine = mine.reshape(ZS, sec_dev * share, cols)
    image = mine[0]
    for dz in range(1, ZS):
        got = lax.ppermute(mine[dz].astype(jnp.bfloat16), "pair", line_perm(dz))
        image = image + got.astype(jnp.float32)
    partial_rows = image.reshape(sec_dev, share, cols).astype(jnp.bfloat16)
    gathered = lax.all_gather(partial_rows, "sec", axis=0, tiled=True)
    summed = pick_sources(gathered, match, targets)
    my_lines = pair * share + jnp.arange(share, dtype=jnp.int32)
    out_keep = my_lines[None, :] < rows_here[:, None]
    return jnp.where(out_keep[:, :, None], summed, jnp.zeros_like(summed))


def solution(mesh):
    in_specs = (
        P("sec", None, None),
        P(),
        P(),
        P("pair", "sec", None, None),
        P("pair", "sec", None, None),
    )
    out_specs = P("sec", "pair", None)
    return jax.shard_map(shards, mesh=mesh, in_specs=in_specs, out_specs=out_specs, check_vma=False)
```

```python
import jax
import jax.numpy as jnp
from jax import lax
from jax.experimental import pallas as pl
from jax.sharding import PartitionSpec as P


INTERPRET = False
YS, ZS, XS = 4, 8, 2
CHUNKS = ((0, 1), (1, 2), (2, 4), (4, 6), (6, 7), (7, 8))
GROUPS = ((0, 1), (2, 3, 4, 5))
SWAPPED = (4,)
F32, BF16 = jnp.float32, jnp.bfloat16


def split_pair(p):
    return p // (ZS * XS), (p // XS) % ZS, p % XS


def join_pair(y, z, x):
    return (y * ZS + z) * XS + x


def perm_of(move):
    return [(p, join_pair(*move(*split_pair(p)))) for p in range(YS * ZS * XS)]


MIRROR = perm_of(lambda y, z, x: (YS - 1 - y, ZS - 1 - z, XS - 1 - x))
STAGES = {
    "a": perm_of(lambda y, z, x: (y ^ 1, z, x)),
    "b": perm_of(lambda y, z, x: (y, z ^ 1, x)),
}


FOURS = {
    "c": (
        perm_of(lambda y, z, x: (y, z, x ^ 1)),
        perm_of(lambda y, z, x: (YS - 1 - y, z, x)),
        perm_of(lambda y, z, x: (YS - 1 - y, z, x ^ 1)),
    ),
    "e": (
        perm_of(lambda y, z, x: (y, z ^ 2, x)),
        perm_of(lambda y, z, x: (y, z ^ 4, x)),
        perm_of(lambda y, z, x: (y, z ^ 6, x)),
    ),
}


def routed_rows(pair, line, share, swapped):
    y, z, x = split_pair(pair)
    a, b, c, e = [(line // (share * n)) % m for n, m in ((32, 2), (16, 2), (4, 4), (1, 4))]
    if swapped:
        a, b = b, a
    near = y ^ a
    owner_y = jnp.where(c >= 2, YS - 1 - near, near)
    return share * join_pair(owner_y, z ^ (b + 2 * e), x ^ (c % 2)) + line % share


def pick_sources(gathered, match, targets):
    total = match.shape[0]
    hits = match[None, :] == targets[:, None]
    source = jnp.sum(jnp.where(hits, jnp.arange(total, dtype=jnp.int32)[None, :], 0), axis=1)
    return gathered[source]


def terms_kernel(half_ref, comp_ref, keep_ref, send_ref):
    rows = keep_ref.shape[1]
    for part, ref in ((1, send_ref), (0, keep_ref)):
        ref[0] = lax.dot_general(
            half_ref[0, part * rows : (part + 1) * rows],
            comp_ref[0],
            (((1,), (1,)), ((), ())),
            preferred_element_type=F32,
        ).astype(ref.dtype)


def terms_of(half, comp, start):
    sectors, cols, _ = comp.shape
    rows = half.shape[1]
    spec = pl.BlockSpec((1, rows // 2, cols), lambda s: (s, 0, 0))
    return pl.pallas_call(
        terms_kernel,
        grid=(sectors,),
        in_specs=[
            pl.BlockSpec((1, rows, cols), lambda s: (s + start, 0, 0)),
            pl.BlockSpec((1, cols, cols), lambda s: (s, 0, 0)),
        ],
        out_specs=[spec, spec],
        out_shape=[
            jax.ShapeDtypeStruct((sectors, rows // 2, cols), F32),
            jax.ShapeDtypeStruct((sectors, rows // 2, cols), BF16),
        ],
        interpret=INTERPRET,
        name="terms",
    )(half, comp)


def exchange(value, perm):
    return lax.ppermute(value, "pair", perm)


def fold(total, got):
    total = total + got.astype(F32)
    cut = total.shape[1] // 2
    return total[:, :cut], total[:, cut:].astype(BF16)


def product(psi, sec_rows, match, normal_ops, comp_ops):
    sec_dev, block_rows, _ = psi.shape
    pairs = lax.axis_size("pair")
    share = block_rows // pairs
    first_sec = lax.axis_index("sec") * sec_dev
    pair = lax.axis_index("pair")
    targets = first_sec + jnp.arange(sec_dev, dtype=jnp.int32)
    rows_here = lax.dynamic_slice_in_dim(sec_rows, first_sec, sec_dev)

    mirrored = [exchange(comp_ops[0, a:b], MIRROR) for a, b in CHUNKS]

    line = jnp.arange(block_rows, dtype=jnp.int32)
    kept = jnp.where((line[None, :] < rows_here[:, None])[:, :, None], psi, jnp.zeros_like(psi))
    half = jnp.einsum("sab,sbc->sac", normal_ops[0], kept, preferred_element_type=F32).astype(BF16)
    routed = []
    for swapped in (False, True):
        rows = routed_rows(pair, line, share, swapped)
        order = (rows[:, None] == line[None, :]).astype(BF16)
        first, end = (CHUNKS[SWAPPED[0]][0], CHUNKS[SWAPPED[-1]][1]) if swapped else (0, sec_dev)
        part = jnp.einsum("ia,sac->sic", order, half[first:end], preferred_element_type=F32)
        routed.append((part.astype(BF16), first))

    flows = []
    for i, (a, _) in enumerate(CHUNKS):
        comp = mirrored[i]
        if i:
            comp, _ = lax.optimization_barrier((comp, flows[-1][1]))
        source, start = routed[i in SWAPPED]
        flows.append(terms_of(source, comp, a - start))
    pieces = []
    for group in GROUPS:
        parts = []
        for i in group:
            keep, send = flows[i]
            near, far = "ba" if i in SWAPPED else "ab"
            got = exchange(send, STAGES[near])
            keep, send = fold(keep, got)
            got = exchange(send, STAGES[far])
            parts.append(keep + got.astype(F32))
        total = jnp.concatenate(parts, axis=0)
        for stage in "ce":
            cut = total.shape[1] // 4
            got = [
                exchange(total[:, (n + 1) * cut : (n + 2) * cut].astype(BF16), FOURS[stage][n])
                for n in range(3)
            ]
            total = total[:, :cut] + sum(value.astype(F32) for value in got)
        pieces.append(total.astype(BF16))

    partial_rows = jnp.concatenate(pieces, axis=0)
    gathered = lax.all_gather(partial_rows, "sec", axis=0, tiled=True)
    summed = pick_sources(gathered, match, targets)
    my_lines = pair * share + jnp.arange(share, dtype=jnp.int32)
    out_keep = my_lines[None, :] < rows_here[:, None]
    return jnp.where(out_keep[:, :, None], summed, jnp.zeros_like(summed))


def solution(mesh):
    in_specs = (
        P("sec", None, None),
        P(),
        P(),
        P("pair", "sec", None, None),
        P("pair", "sec", None, None),
    )
    out_specs = P("sec", "pair", None)
    return jax.shard_map(product, mesh=mesh, in_specs=in_specs, out_specs=out_specs, check_vma=False)
```

```python
import jax
import jax.numpy as jnp
from jax import lax
from jax.experimental import pallas as pl
from jax.sharding import PartitionSpec as P


INTERPRET = False
YS, ZS, XS = 4, 8, 2
CHUNKS = ((0, 1), (1, 2), (2, 4), (4, 6), (6, 7), (7, 8))
GROUPS = ((0, 1), (2, 3), (4, 5))
SWAPPED = (4,)
F32, BF16 = jnp.float32, jnp.bfloat16


def split_pair(p):
    return p // (ZS * XS), (p // XS) % ZS, p % XS


def join_pair(y, z, x):
    return (y * ZS + z) * XS + x


def perm_of(move):
    return [(p, join_pair(*move(*split_pair(p)))) for p in range(YS * ZS * XS)]


MIRROR = perm_of(lambda y, z, x: (YS - 1 - y, ZS - 1 - z, XS - 1 - x))
STAGES = {
    "a": perm_of(lambda y, z, x: (y ^ 1, z, x)),
    "b": perm_of(lambda y, z, x: (y, z ^ 1, x)),
}


FOURS = {
    "c": (
        perm_of(lambda y, z, x: (y, z, x ^ 1)),
        perm_of(lambda y, z, x: (YS - 1 - y, z, x)),
        perm_of(lambda y, z, x: (YS - 1 - y, z, x ^ 1)),
    ),
    "e": (
        perm_of(lambda y, z, x: (y, z ^ 2, x)),
        perm_of(lambda y, z, x: (y, z ^ 4, x)),
        perm_of(lambda y, z, x: (y, z ^ 6, x)),
    ),
}


def routed_rows(pair, line, share, swapped):
    y, z, x = split_pair(pair)
    a, b, c, e = [(line // (share * n)) % m for n, m in ((32, 2), (16, 2), (4, 4), (1, 4))]
    if swapped:
        a, b = b, a
    near = y ^ a
    owner_y = jnp.where(c >= 2, YS - 1 - near, near)
    return share * join_pair(owner_y, z ^ (b + 2 * e), x ^ (c % 2)) + line % share


def pick_sources(gathered, match, targets):
    total = match.shape[0]
    hits = match[None, :] == targets[:, None]
    source = jnp.sum(jnp.where(hits, jnp.arange(total, dtype=jnp.int32)[None, :], 0), axis=1)
    return gathered[source]


def terms_kernel(half_ref, comp_ref, keep_ref, send_ref):
    rows = keep_ref.shape[1]
    for part, ref in ((1, send_ref), (0, keep_ref)):
        ref[0] = lax.dot_general(
            half_ref[0, part * rows : (part + 1) * rows],
            comp_ref[0],
            (((1,), (1,)), ((), ())),
            preferred_element_type=F32,
        ).astype(ref.dtype)


def terms_of(half, comp, start):
    sectors, cols, _ = comp.shape
    rows = half.shape[1]
    spec = pl.BlockSpec((1, rows // 2, cols), lambda s: (s, 0, 0))
    return pl.pallas_call(
        terms_kernel,
        grid=(sectors,),
        in_specs=[
            pl.BlockSpec((1, rows, cols), lambda s: (s + start, 0, 0)),
            pl.BlockSpec((1, cols, cols), lambda s: (s, 0, 0)),
        ],
        out_specs=[spec, spec],
        out_shape=[
            jax.ShapeDtypeStruct((sectors, rows // 2, cols), F32),
            jax.ShapeDtypeStruct((sectors, rows // 2, cols), BF16),
        ],
        interpret=INTERPRET,
        name="terms",
    )(half, comp)


def part_kernel(half_ref, comp_ref, out_ref):
    out_ref[0] = lax.dot_general(
        half_ref[0], comp_ref[0], (((1,), (1,)), ((), ())), preferred_element_type=F32
    ).astype(out_ref.dtype)


def part_of(half, comp, start, part, dtype):
    sectors, cols, _ = comp.shape
    rows = half.shape[1] // 2
    return pl.pallas_call(
        part_kernel,
        grid=(sectors,),
        in_specs=[
            pl.BlockSpec((1, rows, cols), lambda s: (s + start, part, 0)),
            pl.BlockSpec((1, cols, cols), lambda s: (s, 0, 0)),
        ],
        out_specs=pl.BlockSpec((1, rows, cols), lambda s: (s, 0, 0)),
        out_shape=jax.ShapeDtypeStruct((sectors, rows, cols), dtype),
        interpret=INTERPRET,
        name="part",
    )(half, comp)


def exchange(value, perm):
    return lax.ppermute(value, "pair", perm)


def fold(total, got):
    total = total + got.astype(F32)
    cut = total.shape[1] // 2
    return total[:, :cut], total[:, cut:].astype(BF16)


def product(psi, sec_rows, match, normal_ops, comp_ops):
    sec_dev, block_rows, _ = psi.shape
    pairs = lax.axis_size("pair")
    share = block_rows // pairs
    first_sec = lax.axis_index("sec") * sec_dev
    pair = lax.axis_index("pair")
    targets = first_sec + jnp.arange(sec_dev, dtype=jnp.int32)
    rows_here = lax.dynamic_slice_in_dim(sec_rows, first_sec, sec_dev)

    mirrored = []
    blocks, rest = comp_ops[0, : CHUNKS[0][1]], comp_ops[0]
    for i, (a, b) in enumerate(CHUNKS):
        if i:
            blocks = rest[a:b]
        mirrored.append(exchange(blocks, MIRROR))
        if not i:
            rest, _ = lax.optimization_barrier((rest, blocks))

    line = jnp.arange(block_rows, dtype=jnp.int32)
    kept = jnp.where((line[None, :] < rows_here[:, None])[:, :, None], psi, jnp.zeros_like(psi))
    half = jnp.einsum("sab,sbc->sac", normal_ops[0], kept, preferred_element_type=F32).astype(BF16)
    routed = []
    for swapped in (False, True):
        rows = routed_rows(pair, line, share, swapped)
        order = (rows[:, None] == line[None, :]).astype(BF16)
        first, end = (CHUNKS[SWAPPED[0]][0], CHUNKS[SWAPPED[-1]][1]) if swapped else (0, sec_dev)
        part = jnp.einsum("ia,sac->sic", order, half[first:end], preferred_element_type=F32)
        routed.append((part.astype(BF16), first))

    flows = []
    for i, (a, _) in enumerate(CHUNKS):
        comp = mirrored[i]
        if i:
            comp, _ = lax.optimization_barrier((comp, flows[-1][1]))
        source, start = routed[i in SWAPPED]
        if i + 1 < len(CHUNKS):
            flows.append(terms_of(source, comp, a - start))
        else:
            send = part_of(source, comp, a - start, 1, BF16)
    flows.append((part_of(source, comp, a - start, 0, F32), send))
    def swap_four(perms, total):
        cut = total.shape[1] // 4
        got = [
            exchange(total[:, (n + 1) * cut : (n + 2) * cut].astype(BF16), perms[n])
            for n in range(3)
        ]
        return total[:, :cut] + sum(value.astype(F32) for value in got)

    totals = []
    for group in GROUPS:
        parts = []
        for i in group:
            near, far = "ba" if i in SWAPPED else "ab"
            keep, send = flows[i]
            got = exchange(send, STAGES[near])
            keep, send = fold(keep, got)
            got = exchange(send, STAGES[far])
            parts.append(keep + got.astype(F32))
        totals.append(swap_four(FOURS["c"], jnp.concatenate(parts, axis=0)))
    total = swap_four(FOURS["e"], jnp.concatenate(totals, axis=0))
    partial_rows = total.astype(BF16)
    gathered = lax.all_gather(partial_rows, "sec", axis=0, tiled=True)
    summed = pick_sources(gathered, match, targets)
    my_lines = pair * share + jnp.arange(share, dtype=jnp.int32)
    out_keep = my_lines[None, :] < rows_here[:, None]
    return jnp.where(out_keep[:, :, None], summed, jnp.zeros_like(summed))


def solution(mesh):
    in_specs = (
        P("sec", None, None),
        P(),
        P(),
        P("pair", "sec", None, None),
        P("pair", "sec", None, None),
    )
    out_specs = P("sec", "pair", None)
    return jax.shard_map(product, mesh=mesh, in_specs=in_specs, out_specs=out_specs, check_vma=False)
```

```python
import jax
import jax.numpy as jnp
from jax import lax
from jax.experimental import pallas as pl
from jax.sharding import PartitionSpec as P


INTERPRET = False
YS, ZS, XS = 4, 8, 2
CHUNKS = ((0, 1), (1, 2), (2, 4), (4, 6), (6, 7), (7, 8))
GROUPS = ((0, 1), (2, 3), (4, 5))
SWAPPED = (4,)
F32, BF16 = jnp.float32, jnp.bfloat16


def split_pair(p):
    return p // (ZS * XS), (p // XS) % ZS, p % XS


def join_pair(y, z, x):
    return (y * ZS + z) * XS + x


def perm_of(move):
    return [(p, join_pair(*move(*split_pair(p)))) for p in range(YS * ZS * XS)]


MIRROR = perm_of(lambda y, z, x: (YS - 1 - y, ZS - 1 - z, XS - 1 - x))
STAGES = {
    "a": perm_of(lambda y, z, x: (y ^ 1, z, x)),
    "b": perm_of(lambda y, z, x: (y, z ^ 1, x)),
}


FOURS = {
    "c": (
        perm_of(lambda y, z, x: (y, z, x ^ 1)),
        perm_of(lambda y, z, x: (YS - 1 - y, z, x)),
        perm_of(lambda y, z, x: (YS - 1 - y, z, x ^ 1)),
    ),
    "e": (
        perm_of(lambda y, z, x: (y, z ^ 2, x)),
        perm_of(lambda y, z, x: (y, z ^ 4, x)),
        perm_of(lambda y, z, x: (y, z ^ 6, x)),
    ),
}


def routed_rows(pair, line, share, swapped):
    y, z, x = split_pair(pair)
    a, b, c, e = [(line // (share * n)) % m for n, m in ((32, 2), (16, 2), (4, 4), (1, 4))]
    if swapped:
        a, b = b, a
    near = y ^ a
    owner_y = jnp.where(c >= 2, YS - 1 - near, near)
    return share * join_pair(owner_y, z ^ (b + 2 * e), x ^ (c % 2)) + line % share


def pick_sources(gathered, match, targets):
    hits = (match[None, :] == targets[:, None]).astype(gathered.dtype)
    return jnp.einsum("ts,sjc->tjc", hits, gathered, preferred_element_type=F32)


def terms_kernel(half_ref, comp_ref, keep_ref, send_ref):
    rows = keep_ref.shape[1]
    for part, ref in ((1, send_ref), (0, keep_ref)):
        ref[0] = lax.dot_general(
            half_ref[0, part * rows : (part + 1) * rows],
            comp_ref[0],
            (((1,), (1,)), ((), ())),
            preferred_element_type=F32,
        ).astype(ref.dtype)


def terms_of(half, comp, start):
    sectors, cols, _ = comp.shape
    rows = half.shape[1]
    spec = pl.BlockSpec((1, rows // 2, cols), lambda s: (s, 0, 0))
    return pl.pallas_call(
        terms_kernel,
        grid=(sectors,),
        in_specs=[
            pl.BlockSpec((1, rows, cols), lambda s: (s + start, 0, 0)),
            pl.BlockSpec((1, cols, cols), lambda s: (s, 0, 0)),
        ],
        out_specs=[spec, spec],
        out_shape=[
            jax.ShapeDtypeStruct((sectors, rows // 2, cols), F32),
            jax.ShapeDtypeStruct((sectors, rows // 2, cols), BF16),
        ],
        interpret=INTERPRET,
        name="terms",
    )(half, comp)


def exchange(value, perm):
    return lax.ppermute(value, "pair", perm)


def fold(total, got):
    total = total + got.astype(F32)
    cut = total.shape[1] // 2
    return total[:, :cut], total[:, cut:].astype(BF16)


def product(psi, sec_rows, match, normal_ops, comp_ops):
    sec_dev, block_rows, _ = psi.shape
    pairs = lax.axis_size("pair")
    share = block_rows // pairs
    first_sec = lax.axis_index("sec") * sec_dev
    pair = lax.axis_index("pair")
    targets = first_sec + jnp.arange(sec_dev, dtype=jnp.int32)
    rows_here = lax.dynamic_slice_in_dim(sec_rows, first_sec, sec_dev)

    mirrored = []
    blocks, rest = comp_ops[0, : CHUNKS[0][1]], comp_ops[0]
    for i, (a, b) in enumerate(CHUNKS):
        if i:
            blocks = rest[a:b]
        mirrored.append(exchange(blocks, MIRROR))
        if not i:
            rest, _ = lax.optimization_barrier((rest, blocks))

    line = jnp.arange(block_rows, dtype=jnp.int32)
    kept = jnp.where((line[None, :] < rows_here[:, None])[:, :, None], psi, jnp.zeros_like(psi))
    half = jnp.einsum("sab,sbc->sac", normal_ops[0], kept, preferred_element_type=F32).astype(BF16)
    routed = []
    for swapped in (False, True):
        rows = routed_rows(pair, line, share, swapped)
        order = (rows[:, None] == line[None, :]).astype(BF16)
        first, end = (CHUNKS[SWAPPED[0]][0], CHUNKS[SWAPPED[-1]][1]) if swapped else (0, sec_dev)
        part = jnp.einsum("ia,sac->sic", order, half[first:end], preferred_element_type=F32)
        routed.append((part.astype(BF16), first))

    flows = []
    for i, (a, _) in enumerate(CHUNKS):
        comp = mirrored[i]
        if i:
            comp, _ = lax.optimization_barrier((comp, flows[-1][1]))
        source, start = routed[i in SWAPPED]
        flows.append(terms_of(source, comp, a - start))
    def swap_four(perms, total):
        cut = total.shape[1] // 4
        got = [
            exchange(total[:, (n + 1) * cut : (n + 2) * cut].astype(BF16), perms[n])
            for n in range(3)
        ]
        return total[:, :cut] + sum(value.astype(F32) for value in got)

    totals = []
    for group in GROUPS:
        parts = []
        for i in group:
            near, far = "ba" if i in SWAPPED else "ab"
            keep, send = flows[i]
            got = exchange(send, STAGES[near])
            keep, send = fold(keep, got)
            got = exchange(send, STAGES[far])
            parts.append(keep + got.astype(F32))
        totals.append(swap_four(FOURS["c"], jnp.concatenate(parts, axis=0)))
    total = swap_four(FOURS["e"], jnp.concatenate(totals, axis=0))
    partial_rows = total.astype(BF16)
    gathered = lax.all_gather(partial_rows, "sec", axis=0, tiled=True)
    summed = pick_sources(gathered, match, targets)
    my_lines = pair * share + jnp.arange(share, dtype=jnp.int32)
    out_keep = my_lines[None, :] < rows_here[:, None]
    return jnp.where(out_keep[:, :, None], summed, jnp.zeros_like(summed)).astype(BF16)


def solution(mesh):
    in_specs = (
        P("sec", None, None),
        P(),
        P(),
        P("pair", "sec", None, None),
        P("pair", "sec", None, None),
    )
    out_specs = P("sec", "pair", None)
    return jax.shard_map(product, mesh=mesh, in_specs=in_specs, out_specs=out_specs, check_vma=False)
```
